128 devices in a mesh: macro: 8 (over y, core), pool: 16 (over x, z).
Axes of the slice: x: 4, y: 4, z: 4, core: 2. Of those that a mesh axis runs over, the one named last changes fastest.
Arguments:
- panels: bfloat16 [16, 768, 768], P('pool', 'macro'), as said below
- loads: float32 [16, 9, 768], P('pool'), may hold values from -6 to 6
- family: int32 [8192, 1], P(('macro', 'pool')), may hold values from 0 to 15; in each aligned block of 64 rows (0 to 63, 64 to 127, ...) at most 8 rows name the same one
- contact: float32 [8192, 768], P(('macro', 'pool')), may hold values from 0.05 to 8
- strain: float32 [8192, 9], P(('macro', 'pool')), may hold values from -6 to 6
- previous: bfloat16 [8192, 6912], P(('macro', 'pool')), may hold values from -3 to 3
Outputs:
- fluct: bfloat16 [8192, 6912], P(('macro', 'pool'))
- stress: float32 [8192, 9], P(('macro', 'pool'))
- tangent: float32 [8192, 81], P(('macro', 'pool'))
The draws below stay inside these ranges and needn't reach their ends.
Inputs may be any that keep to these rules, and one draw needn't show every extreme that they name: Within the rows of one device no family is named more than 8 times, a bound that some block reaches. `panels`: each panel is symmetric and positive definite.
All inputs are finite; a program needn't handle non-finite values.
Results may differ from the reference program's by a relative error of at most 0.0085.
Values may be sent and summed in bfloat16 or wider, within the bound.
No kernel may reach another device: no remote copies, remote signals or barrier semaphores. Data moves between devices by JAX's collectives and lax.ppermute only.
A program may use at most 64 MiB of HBM per device.

```python
import math
import jax
import jax.numpy as jnp
import numpy as np
from jax import lax

DOF = 768
RHS = 9
ITERS = 4
PT_DEV = 64
CAP = 8
FAMS = 16
POINTS = 8192


def draw_panels(key, part):
    yarn_width = 64
    yarn_index = jnp.arange(DOF, dtype=jnp.int32) // yarn_width
    coupled = (yarn_index[None, :] == yarn_index[:, None]) | (yarn_index[None, :] == yarn_index[:, None] + 1)
    factor = jax.random.normal(key, (FAMS, DOF, DOF), jnp.float32)
    factor = jnp.where(coupled[None, :, :], factor, 0.0)
    product_matrix = jnp.einsum('fik,fjk->fij', factor, factor, precision=lax.Precision.HIGHEST)
    product_matrix = 0.5 * (product_matrix + jnp.swapaxes(product_matrix, 1, 2))
    identity = jnp.eye(DOF, dtype=jnp.float32)
    matrix = product_matrix / (2.0 * yarn_width) + 0.2 * identity[None, :, :]
    return matrix.astype(jnp.bfloat16)


def steps_of(rng, shape, pieces, smallest, high):
    def one(axis_at, parts):
        draws = jax.random.uniform(jax.random.fold_in(jax.random.fold_in(rng, 6), axis_at), (parts,), jnp.float32, smallest / len(pieces), high / len(pieces))
        return jnp.repeat(jnp.exp(draws), shape[axis_at] // parts).reshape((-1,) + (1,) * (len(shape) - axis_at - 1))

    level = one(*pieces[0])
    for cut in pieces[1:]:
        level = level * one(*cut)
    return level


def deal_out(own_key, own, number, rows, amount, top, limit, slope):
    ranking = jax.random.permutation(own_key, amount)
    heavy_load, ordinary = shares(amount, rows * top, limit, slope, True), shares(amount, rows * top, limit, slope, False)
    places = jnp.arange(amount)

    def named(lengths, turn):
        used = int((lengths > 0).sum())
        fixed = max(1, used // 4)
        passed = fixed + (places - fixed + turn * (used - fixed)) % max(1, amount - fixed)
        return jnp.zeros((amount,), jnp.int32).at[ranking[jnp.where(places < fixed, places, passed)]].set(jnp.asarray(lengths, jnp.int32))

    lengths = jnp.where(number % 4 == 0, named(heavy_load, number // 4), named(ordinary, number - number // 4 - 1))
    mixed = jax.random.permutation(jax.random.fold_in(own, 3), amount)
    donor, sink = mixed[0:amount // 2 * 2:2], mixed[1:amount // 2 * 2:2]
    room = jnp.minimum(lengths[donor] - 1, limit - lengths[sink]) // 2
    room = jnp.where((donor == ranking[0]) | (sink == ranking[0]) | (lengths[sink] == 0), 0, jnp.maximum(room, 0))
    passed = jax.random.randint(jax.random.fold_in(own, 4), (amount // 2,), 0, 1 << 20) % (room + 1)
    lengths = lengths.at[donor].add(-passed).at[sink].add(passed)
    members = jnp.searchsorted(jnp.cumsum(lengths), jnp.arange(rows * top), side="right").astype(jnp.int32)
    listing = members.reshape(top, rows).T
    listing = listing[jax.random.permutation(jax.random.fold_in(own, 1), rows)]
    turn = jax.random.randint(jax.random.fold_in(own, 2), (rows, 1), 0, top)
    return jnp.take_along_axis(listing, (jnp.arange(top)[None, :] + turn) % top, axis=1)


def shares(number_of, total, limit, skew, full):
    weights = [(1 << 20) // math.isqrt(grade ** skew) + 1 for grade in range(1, number_of + 1)]
    largest = limit if full else min(limit, max(-(-total // number_of), total * weights[0] // sum(weights)))
    least = 1 if total - largest >= number_of - 1 else 0
    given, surplus = [largest] + [least] * (number_of - 1), total - largest - least * (number_of - 1)
    while surplus > 0:
        movable = [i for i in range(1, number_of) if given[i] < largest] or [i for i in range(1, number_of) if given[i] < limit]
        whole, budget = sum([weights[i] for i in movable]), surplus
        for i in movable:
            extra = min(limit - given[i], max(1, budget * weights[i] // whole), surplus)
            given[i] = given[i] + extra
            surplus = surplus - extra
    return np.array(given)


def bell_draw(rng, extent, scale, bound, pieces=(), kind=jnp.bfloat16):
    loudness = steps_of(rng, extent, pieces, -0.22, 0.18) if pieces else 1.0
    result = jax.random.normal(rng, extent, jnp.float32) * scale * loudness
    return jnp.minimum(jnp.maximum(result, -bound), bound).astype(kind)


def setup_inputs(seed: int = 0) -> dict:
    arg_keys = jax.random.split(jax.random.key(seed), 7)
    panels = draw_panels(jax.random.fold_in(arg_keys[6], 71), 0)
    loads = bell_draw(arg_keys[1], (FAMS, RHS, DOF), 1.0, 6.0, ((0, 16),), jnp.float32)
    family_keys = jax.random.split(jax.random.fold_in(arg_keys[2], 1), POINTS // PT_DEV)
    family_turns = jax.random.permutation(jax.random.fold_in(arg_keys[2], 3), POINTS // PT_DEV)
    family = jax.vmap(lambda own, number: deal_out(jax.random.fold_in(arg_keys[2], 2), own, number, PT_DEV, FAMS, 1, CAP, 2))(family_keys, family_turns).reshape((POINTS, 1))
    contact = jnp.clip(jnp.exp(math.log(8.0) - 5.075174 * jax.random.uniform(arg_keys[3], (POINTS, DOF), jnp.float32) ** steps_of(arg_keys[3], (POINTS, DOF), ((0, 128),), -0.2, 0.2)), 0.05, 8.0)
    strain = bell_draw(arg_keys[4], (POINTS, RHS), 1.0, 6.0, ((0, 128),), jnp.float32)
    previous = bell_draw(arg_keys[5], (POINTS, RHS * DOF), 0.5, 3.0, ((0, 128),))
    return {"panels": panels, "loads": loads, "family": family, "contact": contact, "strain": strain, "previous": previous}


def solve_cells(panel, load, contact_rows, previous_rows, strain_rows):
    cells = contact_rows.shape[0]
    width = panel.shape[0]
    count = load.shape[0]
    stiff = panel.astype(jnp.float32)
    inverse = 1.0 / jnp.diagonal(stiff)

    def apply_stiffness(field):
        flat = field.reshape(cells * count, width)
        product = jnp.dot(flat, stiff, precision=lax.Precision.HIGHEST).reshape(cells, count, width)
        return product + contact_rows[:, None, :] * field

    iterate = previous_rows.astype(jnp.float32).reshape(cells, count, width)
    residual = load[None, :, :] - apply_stiffness(iterate)
    scaled = inverse * residual
    direction = scaled
    current = jnp.sum(residual * scaled, axis=-1)
    for sweep in range(ITERS):
        image = apply_stiffness(direction)
        step_size = current / (jnp.sum(direction * image, axis=-1) + 1e-6)
        iterate = iterate + step_size[:, :, None] * direction
        residual = residual - step_size[:, :, None] * image
        scaled = inverse * residual
        updated = jnp.sum(residual * scaled, axis=-1)
        direction = scaled + (updated / (current + 1e-6))[:, :, None] * direction
        current = updated
    tangent = jnp.einsum("sik,jk->sij", iterate, load, precision=lax.Precision.HIGHEST) / width
    stress = jnp.einsum("sij,sj->si", tangent, strain_rows, precision=lax.Precision.HIGHEST)
    return (iterate.astype(jnp.bfloat16).reshape(cells, count * width), stress,
            tangent.reshape(cells, count * count))


def reference(panels, loads, family, contact, strain, previous):
    def one_point(inputs):
        member, contact_row, strain_row, previous_row = inputs
        panel = lax.dynamic_index_in_dim(panels, member, 0, keepdims=False)
        load = lax.dynamic_index_in_dim(loads, member, 0, keepdims=False)
        new_rows, stress_rows, tangent_rows = solve_cells(
            panel, load, contact_row[None, :], previous_row[None, :], strain_row[None, :])
        return new_rows[0], stress_rows[0], tangent_rows[0]

    fluct, stress, tangent = lax.map(one_point, (family[:, 0], contact, strain, previous))
    return fluct, stress, tangent
```

```python
import jax
import jax.numpy as jnp
from jax import lax
from jax.experimental import pallas as pl
from jax.experimental.pallas import tpu as pltpu
from jax.sharding import PartitionSpec as P

DOF = 768
RHS = 9
ITERS = 4
CAP = 8
LANES = 128


def cells_kernel(spot_ref, load_ref, own_ref, below_ref, above_ref, far_ref, points_ref, out_ref, panel_ref, contact_ref):
    level = spot_ref[0]
    rows = own_ref.shape[0]
    count = DOF // rows
    for step, block in enumerate((own_ref, above_ref, far_ref, below_ref)):
        at = pl.multiple_of(lax.rem(level + step, count) * rows, rows)
        panel_ref[pl.ds(at, rows), :] = block[...]

    eye = lax.broadcasted_iota(jnp.int32, (LANES, LANES), 0) == lax.broadcasted_iota(
        jnp.int32, (LANES, LANES), 1
    )
    pieces = []
    for k in range(DOF // LANES):
        tile = panel_ref[k * LANES : (k + 1) * LANES, k * LANES : (k + 1) * LANES].astype(jnp.float32)
        pieces.append(jnp.sum(jnp.where(eye, tile, 0.0), axis=0, keepdims=True))
    inverse = 1.0 / jnp.concatenate(pieces, axis=1)

    held = points_ref[:, RHS * DOF :].astype(jnp.float32)
    contact_ref[...] = jnp.where(held > 0.0, held, 1.0)

    loads = load_ref[...]
    slots = points_ref.shape[0]
    padded = jnp.concatenate([loads, jnp.zeros((LANES - RHS, DOF), jnp.float32)], axis=0).astype(jnp.bfloat16)
    tangent = jnp.zeros((slots, LANES), jnp.float32)

    def times(field):
        return jnp.dot(field, panel_ref[...], preferred_element_type=jnp.float32)

    for case in range(RHS):
        cols = slice(case * DOF, (case + 1) * DOF)
        start = points_ref[:, cols]
        contact = contact_ref[...]
        iterate = start.astype(jnp.float32)
        residual = loads[case : case + 1, :] - (times(start) + contact * iterate)
        direction = inverse * residual
        current = jnp.sum(residual * direction, axis=1, keepdims=True)
        for sweep in range(ITERS):
            image = times(direction.astype(jnp.bfloat16)) + contact * direction
            step = current / (jnp.sum(direction * image, axis=1, keepdims=True) + 1e-6)
            iterate = iterate + step * direction
            if sweep + 1 < ITERS:
                residual = residual - step * image
                scaled = inverse * residual
                updated = jnp.sum(residual * scaled, axis=1, keepdims=True)
                direction = scaled + (updated / (current + 1e-6)) * direction
                current = updated
        rounded = iterate.astype(jnp.bfloat16)
        out_ref[:, cols] = rounded
        part = lax.dot_general(rounded, padded, (((1,), (1,)), ((), ())), preferred_element_type=jnp.float32)
        tangent = tangent + (pltpu.roll(part, case * RHS, 1) if case else part)
    out_ref[:, RHS * DOF :] = (tangent * (1.0 / DOF)).astype(jnp.bfloat16)


def on_device(panels, loads, family, contact, strain, previous):
    pool = lax.axis_size("pool")
    macro = lax.axis_size("macro")
    points = contact.shape[0]
    me = lax.axis_index("macro")

    own = panels[0]
    other = lax.ppermute(own, "macro", [(i, i ^ 1) for i in range(macro)])
    pair = jnp.where(
        me % 2 == 0,
        jnp.concatenate([own, other], axis=0),
        jnp.concatenate([other, own], axis=0),
    )
    below = lax.ppermute(pair, "macro", [(i, (i + 2) % macro) for i in range(macro)])
    above = lax.ppermute(pair, "macro", [(i, (i - 2) % macro) for i in range(macro)])
    far = lax.ppermute(pair, "macro", [(i, (i + 4) % macro) for i in range(macro)])

    ids = family[:, 0]
    one_hot = (ids[:, None] == jnp.arange(pool, dtype=jnp.int32)[None, :]).astype(jnp.int32)
    rank = jnp.sum(jnp.cumsum(one_hot, axis=0) * one_hot, axis=1) - 1
    slot = ids * CAP + rank
    picking = (slot[None, :] == jnp.arange(pool * CAP, dtype=jnp.int32)[:, None]).astype(jnp.bfloat16)

    def pick(matrix, rows):
        return jnp.dot(matrix, rows, preferred_element_type=jnp.float32).astype(jnp.bfloat16)

    table = jnp.concatenate([previous, contact.astype(jnp.bfloat16)], axis=1)
    sent = pick(picking, table)
    held = lax.all_to_all(sent, "pool", 0, 0, tiled=True)

    vmem = pl.BlockSpec(memory_space=pltpu.VMEM)
    solved = pl.pallas_call(
        cells_kernel,
        out_shape=jax.ShapeDtypeStruct((pool * CAP, RHS * DOF + LANES), jnp.bfloat16),
        in_specs=[pl.BlockSpec(memory_space=pltpu.SMEM)] + [vmem] * 6,
        out_specs=vmem,
        scratch_shapes=[pltpu.VMEM((DOF, DOF), jnp.bfloat16), pltpu.VMEM((pool * CAP, DOF), jnp.float32)],
        compiler_params=pltpu.CompilerParams(vmem_limit_bytes=48 * 2**20),
        name="cells",
    )((me // 2).astype(jnp.int32).reshape(1), loads[0], pair, below, above, far, held)

    back = lax.all_to_all(solved, "pool", 0, 0, tiled=True)
    fluct = pick(picking.T, back[:, : RHS * DOF])
    tangent = jnp.dot(picking.T, back[:, RHS * DOF :], preferred_element_type=jnp.float32)[:, : RHS * RHS]
    stress = jnp.sum(tangent.reshape(points, RHS, RHS) * strain[:, None, :], axis=2)
    return fluct, stress, tangent


def solution(mesh):
    rows = P(("macro", "pool"), None)
    return jax.shard_map(
        on_device,
        mesh=mesh,
        in_specs=(P("pool", "macro", None), P("pool", None, None), rows, rows, rows, rows),
        out_specs=(rows, rows, rows),
        check_vma=False,
    )
```

```python
import jax
import jax.numpy as jnp
from jax import lax
from jax.experimental import pallas as pl
from jax.experimental.pallas import tpu as pltpu
from jax.sharding import PartitionSpec as P

DOF = 768
RHS = 9
ITERS = 4
CAP = 8
LANES = 128
STRIP = 16
SPLIT = 4


VMEM = pl.BlockSpec(memory_space=pltpu.VMEM)
SMEM = pl.BlockSpec(memory_space=pltpu.SMEM)
PARAMS = pltpu.CompilerParams(vmem_limit_bytes=48 * 2**20)


def pick_first_kernel(family_ref, contact_ref, previous_ref, place_ref, sent_ref):
    ids = family_ref[...]
    points = ids.shape[0]
    lane = lax.broadcasted_iota(jnp.int32, (points, LANES), 1)
    member = (ids == lane).astype(jnp.bfloat16)
    earlier = (
        lax.broadcasted_iota(jnp.int32, (points, points), 1)
        < lax.broadcasted_iota(jnp.int32, (points, points), 0)
    ).astype(jnp.bfloat16)
    before = jnp.dot(earlier, member, preferred_element_type=jnp.float32)
    rank = jnp.sum(before * member.astype(jnp.float32), axis=1, keepdims=True)
    place = (ids * CAP + rank.astype(jnp.int32) == lane).astype(jnp.bfloat16)
    place_ref[...] = place
    sent_ref[:, :DOF] = take(place, contact_ref[...].astype(jnp.bfloat16))
    sent_ref[:, DOF:] = take(place, previous_ref[:, : SPLIT * DOF])


def pick_second_kernel(place_ref, previous_ref, sent_ref):
    sent_ref[...] = take(place_ref[...], previous_ref[:, SPLIT * DOF :])


def take(place, rows):
    return lax.dot_general(place, rows, (((0,), (0,)), ((), ())), preferred_element_type=jnp.float32).astype(
        jnp.bfloat16
    )


def cells(cases, panel_ref, inverse_ref, load_ref, contact_ref, points_ref, offset, out_ref, x_ref, r_ref, d_ref, db_ref, p_ref):
    slots = points_ref.shape[0]
    padded = jnp.concatenate([load_ref[...], jnp.zeros((LANES - RHS, DOF), jnp.float32)], axis=0).astype(
        jnp.bfloat16
    )
    parts = []

    def solve(number, case):
        base = number * slots
        into = slice(number * DOF, (number + 1) * DOF)
        held = slice(offset + number * DOF, offset + (number + 1) * DOF)
        whole = slice(base, base + slots)
        p_ref[whole, :] = jnp.dot(points_ref[:, held], panel_ref[...], preferred_element_type=jnp.float32)
        yield
        currents = []
        for s in range(0, slots, STRIP):
            at = slice(base + s, base + s + STRIP)
            here = slice(s, s + STRIP)
            x = points_ref[here, held].astype(jnp.float32)
            r = load_ref[case : case + 1, :] - (p_ref[at, :] + contact_ref[here, :] * x)
            d = inverse_ref[...] * r
            currents.append(jnp.sum(r * d, axis=1, keepdims=True))
            r_ref[at, :] = r
            d_ref[at, :] = d
            db_ref[at, :] = d.astype(jnp.bfloat16)
        for sweep in range(ITERS):
            p_ref[whole, :] = jnp.dot(db_ref[whole, :], panel_ref[...], preferred_element_type=jnp.float32)
            yield
            for n, s in enumerate(range(0, slots, STRIP)):
                at = slice(base + s, base + s + STRIP)
                here = slice(s, s + STRIP)
                d = d_ref[at, :]
                image = p_ref[at, :] + contact_ref[here, :] * d
                current = currents[n]
                step = current / (jnp.sum(d * image, axis=1, keepdims=True) + 1e-6)
                x = points_ref[here, held].astype(jnp.float32) if sweep == 0 else x_ref[at, :]
                x = x + step * d
                if sweep + 1 == ITERS:
                    out_ref[here, into] = x.astype(jnp.bfloat16)
                    continue
                x_ref[at, :] = x
                r = r_ref[at, :] - step * image
                scaled = inverse_ref[...] * r
                updated = jnp.sum(r * scaled, axis=1, keepdims=True)
                d = scaled + (updated / (current + 1e-6)) * d
                if sweep + 2 < ITERS:
                    r_ref[at, :] = r
                d_ref[at, :] = d
                db_ref[at, :] = d.astype(jnp.bfloat16)
                currents[n] = updated
        part = lax.dot_general(
            out_ref[:, into], padded, (((1,), (1,)), ((), ())), preferred_element_type=jnp.float32
        )
        parts.append(pltpu.roll(part, case * RHS, 1) if case else part)
        yield

    running = [solve(number, case) for number, case in enumerate(cases)]
    while running:
        running = [one for one in running if next(one, running) is not running]
    return sum(parts[1:], parts[0])


def first_kernel(spot_ref, load_ref, own_ref, above_ref, far_ref, below_ref, points_ref,
                 out_ref, tangent_ref, panel_ref, inverse_ref, contact_ref, *work):
    rows = own_ref.shape[0]
    count = DOF // rows
    for step, block in enumerate((own_ref, above_ref, far_ref, below_ref)):
        at = pl.multiple_of(lax.rem(spot_ref[0] + step, count) * rows, rows)
        panel_ref[pl.ds(at, rows), :] = block[...]
    eye = lax.broadcasted_iota(jnp.int32, (LANES, LANES), 0) == lax.broadcasted_iota(
        jnp.int32, (LANES, LANES), 1
    )
    pieces = []
    for k in range(DOF // LANES):
        tile = panel_ref[k * LANES : (k + 1) * LANES, k * LANES : (k + 1) * LANES].astype(jnp.float32)
        pieces.append(jnp.sum(jnp.where(eye, tile, 0.0), axis=0, keepdims=True))
    inverse_ref[...] = 1.0 / jnp.concatenate(pieces, axis=1)
    held = points_ref[:, :DOF].astype(jnp.float32)
    contact_ref[...] = jnp.where(held > 0.0, held, 1.0)
    tangent_ref[...] = cells(range(SPLIT), panel_ref, inverse_ref, load_ref, contact_ref, points_ref, DOF, out_ref, *work)


def second_kernel(load_ref, panel_ref, inverse_ref, contact_ref, tangent_ref, points_ref, out_ref, *work):
    total = tangent_ref[...] + cells(
        range(SPLIT, RHS), panel_ref, inverse_ref, load_ref, contact_ref, points_ref, 0, out_ref, *work
    )
    out_ref[:, (RHS - SPLIT) * DOF :] = (total * (1.0 / DOF)).astype(jnp.bfloat16)


def put_kernel(place_ref, strain_ref, first_ref, second_ref, fluct_ref, stress_ref, tangent_ref):
    place = place_ref[...]

    def put(rows):
        return jnp.dot(place, rows, preferred_element_type=jnp.float32)

    cut = SPLIT * DOF
    fluct_ref[:, :cut] = put(first_ref[...]).astype(jnp.bfloat16)
    fluct_ref[:, cut:] = put(second_ref[:, : RHS * DOF - cut]).astype(jnp.bfloat16)
    tangent = put(second_ref[:, RHS * DOF - cut :])
    entry = lax.broadcasted_iota(jnp.int32, (RHS, LANES), 1)
    index = lax.broadcasted_iota(jnp.int32, (RHS, LANES), 0)
    inside = entry < RHS * RHS
    spread = (inside & (lax.rem(entry, RHS) == index)).astype(jnp.float32)
    gather = (inside & (lax.div(entry, RHS) == index)).astype(jnp.float32)
    strain = jnp.dot(strain_ref[...], spread, precision=lax.Precision.HIGHEST)
    stress_ref[...] = lax.dot_general(
        tangent * strain, gather, (((1,), (1,)), ((), ())), precision=lax.Precision.HIGHEST
    )
    tangent_ref[...] = tangent[:, : RHS * RHS]


def work(cases, slots):
    rows = cases * slots
    return [pltpu.VMEM((rows, DOF), jnp.float32)] * 3 + [
        pltpu.VMEM((rows, DOF), jnp.bfloat16),
        pltpu.VMEM((rows, DOF), jnp.float32),
    ]


def on_device(panels, loads, family, contact, strain, previous):
    pool = lax.axis_size("pool")
    macro = lax.axis_size("macro")
    points = contact.shape[0]
    slots = pool * CAP
    me = lax.axis_index("macro")
    bf16, f32 = jnp.bfloat16, jnp.float32

    def swap(values):
        return lax.all_to_all(values, "pool", 0, 0, tiled=True)

    place, sent = pl.pallas_call(
        pick_first_kernel,
        out_shape=(
            jax.ShapeDtypeStruct((points, slots), bf16),
            jax.ShapeDtypeStruct((slots, (1 + SPLIT) * DOF), bf16),
        ),
        in_specs=[VMEM] * 3,
        out_specs=(VMEM, VMEM),
        compiler_params=PARAMS,
        name="pick_first",
    )(family, contact, previous)
    held_first = swap(sent)
    sent = pl.pallas_call(
        pick_second_kernel,
        out_shape=jax.ShapeDtypeStruct((slots, (RHS - SPLIT) * DOF), bf16),
        in_specs=[VMEM] * 2,
        out_specs=VMEM,
        compiler_params=PARAMS,
        name="pick_second",
    )(place, previous)
    held_second = swap(sent)

    own = panels[0]
    other = lax.ppermute(own, "macro", [(i, i ^ 1) for i in range(macro)])
    pair = jnp.where(
        me % 2 == 0,
        jnp.concatenate([own, other], axis=0),
        jnp.concatenate([other, own], axis=0),
    )
    below, above, far = (
        lax.ppermute(pair, "macro", [(i, (i + shift) % macro) for i in range(macro)]) for shift in (2, -2, 4)
    )

    back_first, tangent, panel, inverse, held_contact = pl.pallas_call(
        first_kernel,
        out_shape=(
            jax.ShapeDtypeStruct((slots, SPLIT * DOF), bf16),
            jax.ShapeDtypeStruct((slots, LANES), f32),
            jax.ShapeDtypeStruct((DOF, DOF), bf16),
            jax.ShapeDtypeStruct((1, DOF), f32),
            jax.ShapeDtypeStruct((slots, DOF), f32),
        ),
        in_specs=[SMEM] + [VMEM] * 6,
        out_specs=(VMEM,) * 5,
        scratch_shapes=work(SPLIT, slots),
        compiler_params=PARAMS,
        name="cells_first",
    )((me // 2).astype(jnp.int32).reshape(1), loads[0], pair, above, far, below, held_first)
    back_first = swap(back_first)
    back_second = swap(
        pl.pallas_call(
            second_kernel,
            out_shape=jax.ShapeDtypeStruct((slots, (RHS - SPLIT) * DOF + LANES), bf16),
            in_specs=[VMEM] * 6,
            out_specs=VMEM,
            scratch_shapes=work(RHS - SPLIT, slots),
            compiler_params=PARAMS,
            name="cells_second",
        )(loads[0], panel, inverse, held_contact, tangent, held_second)
    )
    return pl.pallas_call(
        put_kernel,
        out_shape=(
            jax.ShapeDtypeStruct((points, RHS * DOF), bf16),
            jax.ShapeDtypeStruct((points, RHS), f32),
            jax.ShapeDtypeStruct((points, RHS * RHS), f32),
        ),
        in_specs=[VMEM] * 4,
        out_specs=(VMEM,) * 3,
        compiler_params=PARAMS,
        name="put",
    )(place, strain, back_first, back_second)


def solution(mesh):
    rows = P(("macro", "pool"), None)
    return jax.shard_map(
        on_device,
        mesh=mesh,
        in_specs=(P("pool", "macro", None), P("pool", None, None), rows, rows, rows, rows),
        out_specs=(rows, rows, rows),
        check_vma=False,
    )
```

```python
import jax
import jax.numpy as jnp
from jax import lax
from jax.experimental import pallas as pl
from jax.experimental.pallas import tpu as pltpu
from jax.sharding import PartitionSpec as P

DOF = 768
RHS = 9
ITERS = 4
CAP = 8
LANES = 128
STRIP = 16
TOGETHER = 3
CHUNKS = 3


VMEM = pl.BlockSpec(memory_space=pltpu.VMEM)
HBM = pl.BlockSpec(memory_space=pltpu.HBM)
SMEM = pl.BlockSpec(memory_space=pltpu.SMEM)
PARAMS = pltpu.CompilerParams(vmem_limit_bytes=48 * 2**20)


def pick_kernel(family_ref, contact_hbm, previous_hbm, place_ref, sent_hbm, contact_ref, previous_ref, sent_ref, sems):
    width = RHS * DOF // CHUNKS
    blocks = [slice(k * width, (k + 1) * width) for k in range(CHUNKS)]
    reads = [pltpu.make_async_copy(contact_hbm, contact_ref, sems.at[0])] + [
        pltpu.make_async_copy(previous_hbm.at[:, block], previous_ref.at[:, block], sems.at[1 + k])
        for k, block in enumerate(blocks)
    ]
    for copy in reads:
        copy.start()
    ids = family_ref[...]
    points = ids.shape[1]
    slots = place_ref.shape[0]
    families = slots // CAP
    member = (ids == lax.broadcasted_iota(jnp.int32, (families, points), 0)).astype(jnp.bfloat16)
    earlier = (
        lax.broadcasted_iota(jnp.int32, (points, points), 0)
        < lax.broadcasted_iota(jnp.int32, (points, points), 1)
    ).astype(jnp.bfloat16)
    before = jnp.dot(member, earlier, preferred_element_type=jnp.float32)
    rank = jnp.sum(before * member.astype(jnp.float32), axis=0, keepdims=True)
    slot = ids * CAP + rank.astype(jnp.int32)
    place = (slot == lax.broadcasted_iota(jnp.int32, (slots, points), 0)).astype(jnp.bfloat16)
    place_ref[...] = place

    def take(rows):
        return jnp.dot(place, rows, preferred_element_type=jnp.float32).astype(jnp.bfloat16)

    writes = []
    for k, copy in enumerate(reads):
        copy.wait()
        if k == 0:
            cols = slice(RHS * DOF, (RHS + 1) * DOF)
            sent_ref[:, cols] = take(contact_ref[...].astype(jnp.bfloat16))
        else:
            cols = blocks[k - 1]
            sent_ref[:, cols] = take(previous_ref[:, cols])
        write = pltpu.make_async_copy(sent_ref.at[:, cols], sent_hbm.at[:, cols], sems.at[1 + CHUNKS + k])
        write.start()
        writes.append(write)
    for write in writes:
        write.wait()


def cells_kernel(spot_ref, load_ref, own_ref, above_ref, far_ref, below_ref, points_ref, out_ref,
                 panel_ref, inverse_ref, contact_ref, x_ref, r_ref, d_ref, db_ref, p_ref):
    rows = own_ref.shape[0]
    count = DOF // rows
    for step, block in enumerate((own_ref, above_ref, far_ref, below_ref)):
        at = pl.multiple_of(lax.rem(spot_ref[0] + step, count) * rows, rows)
        panel_ref[pl.ds(at, rows), :] = block[...]
    eye = lax.broadcasted_iota(jnp.int32, (LANES, LANES), 0) == lax.broadcasted_iota(
        jnp.int32, (LANES, LANES), 1
    )
    pieces = []
    for k in range(DOF // LANES):
        tile = panel_ref[k * LANES : (k + 1) * LANES, k * LANES : (k + 1) * LANES].astype(jnp.float32)
        pieces.append(jnp.sum(jnp.where(eye, tile, 0.0), axis=0, keepdims=True))
    inverse_ref[...] = 1.0 / jnp.concatenate(pieces, axis=1)
    held = points_ref[:, RHS * DOF :].astype(jnp.float32)
    contact_ref[...] = jnp.where(held > 0.0, held, 1.0)
    slots = points_ref.shape[0]
    padded = jnp.concatenate([load_ref[...], jnp.zeros((LANES - RHS, DOF), jnp.float32)], axis=0).astype(
        jnp.bfloat16
    )
    parts = []

    def solve(case):
        base = case * slots
        cols = slice(case * DOF, (case + 1) * DOF)
        whole = slice(base, base + slots)
        p_ref[whole, :] = jnp.dot(points_ref[:, cols], panel_ref[...], preferred_element_type=jnp.float32)
        yield
        currents = []
        for s in range(0, slots, STRIP):
            at = slice(base + s, base + s + STRIP)
            here = slice(s, s + STRIP)
            x = points_ref[here, cols].astype(jnp.float32)
            r = load_ref[case : case + 1, :] - (p_ref[at, :] + contact_ref[here, :] * x)
            d = inverse_ref[...] * r
            currents.append(jnp.sum(r * d, axis=1, keepdims=True))
            r_ref[at, :] = r
            d_ref[at, :] = d
            db_ref[at, :] = d.astype(jnp.bfloat16)
        for sweep in range(ITERS):
            p_ref[whole, :] = jnp.dot(db_ref[whole, :], panel_ref[...], preferred_element_type=jnp.float32)
            yield
            for n, s in enumerate(range(0, slots, STRIP)):
                at = slice(base + s, base + s + STRIP)
                here = slice(s, s + STRIP)
                d = d_ref[at, :]
                image = p_ref[at, :] + contact_ref[here, :] * d
                current = currents[n]
                step = current / (jnp.sum(d * image, axis=1, keepdims=True) + 1e-6)
                x = points_ref[here, cols].astype(jnp.float32) if sweep == 0 else x_ref[at, :]
                x = x + step * d
                if sweep + 1 == ITERS:
                    out_ref[here, cols] = x.astype(jnp.bfloat16)
                    continue
                x_ref[at, :] = x
                r = r_ref[at, :] - step * image
                scaled = inverse_ref[...] * r
                updated = jnp.sum(r * scaled, axis=1, keepdims=True)
                d = scaled + (updated / (current + 1e-6)) * d
                if sweep + 2 < ITERS:
                    r_ref[at, :] = r
                d_ref[at, :] = d
                db_ref[at, :] = d.astype(jnp.bfloat16)
                currents[n] = updated
        part = lax.dot_general(
            out_ref[:, cols], padded, (((1,), (1,)), ((), ())), preferred_element_type=jnp.float32
        )
        parts.append(pltpu.roll(part, case * RHS, 1) if case else part)
        yield

    for first in range(0, RHS, TOGETHER):
        running = [solve(case) for case in range(first, min(first + TOGETHER, RHS))]
        while running:
            running = [one for one in running if next(one, running) is not running]
    out_ref[:, RHS * DOF :] = (sum(parts[1:], parts[0]) * (1.0 / DOF)).astype(jnp.bfloat16)


def put_kernel(place_ref, strain_ref, back_ref, fluct_ref, stress_ref, tangent_ref):
    place = place_ref[...]

    def put(rows):
        return lax.dot_general(place, rows, (((0,), (0,)), ((), ())), preferred_element_type=jnp.float32)

    fluct_ref[...] = put(back_ref[:, : RHS * DOF]).astype(jnp.bfloat16)
    tangent = put(back_ref[:, RHS * DOF :])
    entry = lax.broadcasted_iota(jnp.int32, (RHS, LANES), 1)
    index = lax.broadcasted_iota(jnp.int32, (RHS, LANES), 0)
    inside = entry < RHS * RHS
    spread = (inside & (lax.rem(entry, RHS) == index)).astype(jnp.float32)
    gather = (inside & (lax.div(entry, RHS) == index)).astype(jnp.float32)
    strain = lax.dot_general(strain_ref[...], spread, (((0,), (0,)), ((), ())), precision=lax.Precision.HIGHEST)
    stress_ref[...] = lax.dot_general(
        gather, tangent * strain, (((1,), (1,)), ((), ())), precision=lax.Precision.HIGHEST
    )
    tangent_ref[...] = tangent[:, : RHS * RHS]


def on_device(panels, loads, family, contact, strain, previous):
    pool = lax.axis_size("pool")
    macro = lax.axis_size("macro")
    points = contact.shape[0]
    slots = pool * CAP
    me = lax.axis_index("macro")
    bf16, f32 = jnp.bfloat16, jnp.float32

    own = panels[0]
    other = lax.ppermute(own, "macro", [(i, i ^ 1) for i in range(macro)])
    pair = jnp.where(
        me % 2 == 0,
        jnp.concatenate([own, other], axis=0),
        jnp.concatenate([other, own], axis=0),
    )
    below, above, far = (
        lax.ppermute(pair, "macro", [(i, (i + shift) % macro) for i in range(macro)]) for shift in (2, -2, 4)
    )

    width = RHS * DOF
    place, sent = pl.pallas_call(
        pick_kernel,
        out_shape=(
            jax.ShapeDtypeStruct((slots, points), bf16),
            jax.ShapeDtypeStruct((slots, width + DOF), bf16),
        ),
        in_specs=[VMEM, HBM, HBM],
        out_specs=(VMEM, HBM),
        scratch_shapes=[
            pltpu.VMEM((points, DOF), f32),
            pltpu.VMEM((points, width), bf16),
            pltpu.VMEM((slots, width + DOF), bf16),
            pltpu.SemaphoreType.DMA((2 * (1 + CHUNKS),)),
        ],
        compiler_params=PARAMS,
        name="pick",
    )(family.reshape(1, points), contact, previous)
    held = lax.all_to_all(sent, "pool", 0, 0, tiled=True)

    rows = RHS * slots
    solved = pl.pallas_call(
        cells_kernel,
        out_shape=jax.ShapeDtypeStruct((slots, width + LANES), bf16),
        in_specs=[SMEM] + [VMEM] * 6,
        out_specs=VMEM,
        scratch_shapes=[
            pltpu.VMEM((DOF, DOF), bf16),
            pltpu.VMEM((1, DOF), f32),
            pltpu.VMEM((slots, DOF), f32),
            pltpu.VMEM((rows, DOF), f32),
            pltpu.VMEM((rows, DOF), f32),
            pltpu.VMEM((rows, DOF), f32),
            pltpu.VMEM((rows, DOF), bf16),
            pltpu.VMEM((rows, DOF), f32),
        ],
        compiler_params=PARAMS,
        name="cells",
    )((me // 2).astype(jnp.int32).reshape(1), loads[0], pair, above, far, below, held)

    back = lax.all_to_all(solved, "pool", 0, 0, tiled=True)
    fluct, stress, tangent = pl.pallas_call(
        put_kernel,
        out_shape=(
            jax.ShapeDtypeStruct((points, width), bf16),
            jax.ShapeDtypeStruct((RHS, points), f32),
            jax.ShapeDtypeStruct((points, RHS * RHS), f32),
        ),
        in_specs=[VMEM] * 3,
        out_specs=(VMEM,) * 3,
        compiler_params=PARAMS,
        name="put",
    )(place, strain.T, back)
    return fluct, stress.T, tangent


def solution(mesh):
    rows = P(("macro", "pool"), None)
    return jax.shard_map(
        on_device,
        mesh=mesh,
        in_specs=(P("pool", "macro", None), P("pool", None, None), rows, rows, rows, rows),
        out_specs=(rows, rows, rows),
        check_vma=False,
    )
```

```python
import jax
import jax.numpy as jnp
from jax import lax
from jax.experimental import pallas as pl
from jax.experimental.pallas import tpu as pltpu
from jax.sharding import PartitionSpec as P

DOF = 768
RHS = 9
ITERS = 4
CAP = 8
LANES = 128
STRIP = 16
TOGETHER = 3
CHUNKS = 3


VMEM = pl.BlockSpec(memory_space=pltpu.VMEM)
HBM = pl.BlockSpec(memory_space=pltpu.HBM)
SMEM = pl.BlockSpec(memory_space=pltpu.SMEM)
PARAMS = pltpu.CompilerParams(vmem_limit_bytes=48 * 2**20)


def pick_kernel(family_hbm, contact_hbm, previous_hbm, place_ref, sent_hbm,
                contact_ref, previous_ref, sent_ref, family_ref, sems):
    width = RHS * DOF // CHUNKS
    blocks = [slice(k * width, (k + 1) * width) for k in range(CHUNKS)]
    reads = [pltpu.make_async_copy(contact_hbm, contact_ref, sems.at[0])] + [
        pltpu.make_async_copy(previous_hbm.at[:, block], previous_ref.at[:, block], sems.at[1 + k])
        for k, block in enumerate(blocks)
    ]
    named = pltpu.make_async_copy(family_hbm, family_ref, sems.at[2 * (1 + CHUNKS)])
    named.start()
    for copy in reads:
        copy.start()
    named.wait()
    ids = family_ref[...]
    points = ids.shape[1]
    slots = place_ref.shape[0]
    families = slots // CAP
    member = (ids == lax.broadcasted_iota(jnp.int32, (families, points), 0)).astype(jnp.bfloat16)
    earlier = (
        lax.broadcasted_iota(jnp.int32, (points, points), 0)
        < lax.broadcasted_iota(jnp.int32, (points, points), 1)
    ).astype(jnp.bfloat16)
    before = jnp.dot(member, earlier, preferred_element_type=jnp.float32)
    rank = jnp.sum(before * member.astype(jnp.float32), axis=0, keepdims=True)
    slot = ids * CAP + rank.astype(jnp.int32)
    place = (slot == lax.broadcasted_iota(jnp.int32, (slots, points), 0)).astype(jnp.bfloat16)
    place_ref[...] = place

    def take(rows):
        return jnp.dot(place, rows, preferred_element_type=jnp.float32).astype(jnp.bfloat16)

    writes = []
    for k, copy in enumerate(reads):
        copy.wait()
        if k == 0:
            cols = slice(RHS * DOF, (RHS + 1) * DOF)
            sent_ref[:, cols] = take(contact_ref[...].astype(jnp.bfloat16))
        else:
            cols = blocks[k - 1]
            sent_ref[:, cols] = take(previous_ref[:, cols])
        write = pltpu.make_async_copy(sent_ref.at[:, cols], sent_hbm.at[:, cols], sems.at[1 + CHUNKS + k])
        write.start()
        writes.append(write)
    for write in writes:
        write.wait()


def cells_kernel(spot_ref, load_ref, own_ref, above_ref, far_ref, below_ref, points_ref, out_ref,
                 panel_ref, inverse_ref, contact_ref, x_ref, r_ref, d_ref, db_ref, p_ref):
    rows = own_ref.shape[0]
    count = DOF // rows
    for step, block in enumerate((own_ref, above_ref, far_ref, below_ref)):
        at = pl.multiple_of(lax.rem(spot_ref[0] + step, count) * rows, rows)
        panel_ref[pl.ds(at, rows), :] = block[...]
    eye = lax.broadcasted_iota(jnp.int32, (LANES, LANES), 0) == lax.broadcasted_iota(
        jnp.int32, (LANES, LANES), 1
    )
    pieces = []
    for k in range(DOF // LANES):
        tile = panel_ref[k * LANES : (k + 1) * LANES, k * LANES : (k + 1) * LANES].astype(jnp.float32)
        pieces.append(jnp.sum(jnp.where(eye, tile, 0.0), axis=0, keepdims=True))
    inverse_ref[...] = 1.0 / jnp.concatenate(pieces, axis=1)
    held = points_ref[:, RHS * DOF :].astype(jnp.float32)
    contact_ref[...] = jnp.where(held > 0.0, held, 1.0)
    slots = points_ref.shape[0]
    padded = jnp.concatenate([load_ref[...], jnp.zeros((LANES - RHS, DOF), jnp.float32)], axis=0).astype(
        jnp.bfloat16
    )
    parts = []

    def solve(case):
        base = case * slots
        cols = slice(case * DOF, (case + 1) * DOF)
        whole = slice(base, base + slots)
        p_ref[whole, :] = jnp.dot(points_ref[:, cols], panel_ref[...], preferred_element_type=jnp.float32)
        yield
        currents = []
        for s in range(0, slots, STRIP):
            at = slice(base + s, base + s + STRIP)
            here = slice(s, s + STRIP)
            x = points_ref[here, cols].astype(jnp.float32)
            r = load_ref[case : case + 1, :] - (p_ref[at, :] + contact_ref[here, :] * x)
            d = inverse_ref[...] * r
            currents.append(jnp.sum(r * d, axis=1, keepdims=True))
            r_ref[at, :] = r
            d_ref[at, :] = d
            db_ref[at, :] = d.astype(jnp.bfloat16)
        for sweep in range(ITERS):
            p_ref[whole, :] = jnp.dot(db_ref[whole, :], panel_ref[...], preferred_element_type=jnp.float32)
            yield
            for n, s in enumerate(range(0, slots, STRIP)):
                at = slice(base + s, base + s + STRIP)
                here = slice(s, s + STRIP)
                d = d_ref[at, :]
                image = p_ref[at, :] + contact_ref[here, :] * d
                current = currents[n]
                step = current / (jnp.sum(d * image, axis=1, keepdims=True) + 1e-6)
                x = points_ref[here, cols].astype(jnp.float32) if sweep == 0 else x_ref[at, :]
                x = x + step * d
                if sweep + 1 == ITERS:
                    out_ref[here, cols] = x.astype(jnp.bfloat16)
                    continue
                x_ref[at, :] = x
                r = r_ref[at, :] - step * image
                scaled = inverse_ref[...] * r
                updated = jnp.sum(r * scaled, axis=1, keepdims=True)
                d = scaled + (updated / (current + 1e-6)) * d
                if sweep + 2 < ITERS:
                    r_ref[at, :] = r
                d_ref[at, :] = d
                db_ref[at, :] = d.astype(jnp.bfloat16)
                currents[n] = updated
        part = lax.dot_general(
            out_ref[:, cols], padded, (((1,), (1,)), ((), ())), preferred_element_type=jnp.float32
        )
        parts.append(pltpu.roll(part, case * RHS, 1) if case else part)
        yield

    for first in range(0, RHS, TOGETHER):
        running = [solve(case) for case in range(first, min(first + TOGETHER, RHS))]
        while running:
            running = [one for one in running if next(one, running) is not running]
    out_ref[:, RHS * DOF :] = (sum(parts[1:], parts[0]) * (1.0 / DOF)).astype(jnp.bfloat16)


def put_kernel(place_ref, strain_ref, back_ref, fluct_ref, stress_ref, tangent_ref):
    place = place_ref[...]

    def put(rows):
        return lax.dot_general(place, rows, (((0,), (0,)), ((), ())), preferred_element_type=jnp.float32)

    fluct_ref[...] = put(back_ref[:, : RHS * DOF]).astype(jnp.bfloat16)
    tangent = put(back_ref[:, RHS * DOF :])
    entry = lax.broadcasted_iota(jnp.int32, (RHS, LANES), 1)
    index = lax.broadcasted_iota(jnp.int32, (RHS, LANES), 0)
    inside = entry < RHS * RHS
    spread = (inside & (lax.rem(entry, RHS) == index)).astype(jnp.float32)
    gather = (inside & (lax.div(entry, RHS) == index)).astype(jnp.float32)
    strain = lax.dot_general(strain_ref[...], spread, (((0,), (0,)), ((), ())), precision=lax.Precision.HIGHEST)
    stress_ref[...] = lax.dot_general(
        gather, tangent * strain, (((1,), (1,)), ((), ())), precision=lax.Precision.HIGHEST
    )
    tangent_ref[...] = tangent[:, : RHS * RHS]


def far_away(values):
    return pltpu.with_memory_space_constraint(values, pltpu.HBM)


def on_device(panels, loads, family, contact, strain, previous):
    pool = lax.axis_size("pool")
    macro = lax.axis_size("macro")
    points = contact.shape[0]
    slots = pool * CAP
    me = lax.axis_index("macro")
    bf16, f32 = jnp.bfloat16, jnp.float32

    own = panels[0]
    other = lax.ppermute(own, "macro", [(i, i ^ 1) for i in range(macro)])
    pair = jnp.where(
        me % 2 == 0,
        jnp.concatenate([own, other], axis=0),
        jnp.concatenate([other, own], axis=0),
    )
    below, above, far = (
        lax.ppermute(pair, "macro", [(i, (i + shift) % macro) for i in range(macro)]) for shift in (2, -2, 4)
    )

    width = RHS * DOF
    place, sent = pl.pallas_call(
        pick_kernel,
        out_shape=(
            jax.ShapeDtypeStruct((slots, points), bf16),
            pltpu.HBM((slots, width + DOF), bf16),
        ),
        in_specs=[HBM, HBM, HBM],
        out_specs=(VMEM, HBM),
        scratch_shapes=[
            pltpu.VMEM((points, DOF), f32),
            pltpu.VMEM((points, width), bf16),
            pltpu.VMEM((slots, width + DOF), bf16),
            pltpu.VMEM((1, points), jnp.int32),
            pltpu.SemaphoreType.DMA((2 * (1 + CHUNKS) + 1,)),
        ],
        compiler_params=PARAMS,
        name="pick",
    )(far_away(family.reshape(1, points)), far_away(contact), far_away(previous))
    held = lax.all_to_all(sent, "pool", 0, 0, tiled=True)

    rows = RHS * slots
    solved = pl.pallas_call(
        cells_kernel,
        out_shape=jax.ShapeDtypeStruct((slots, width + LANES), bf16),
        in_specs=[SMEM] + [VMEM] * 6,
        out_specs=VMEM,
        scratch_shapes=[
            pltpu.VMEM((DOF, DOF), bf16),
            pltpu.VMEM((1, DOF), f32),
            pltpu.VMEM((slots, DOF), f32),
            pltpu.VMEM((rows, DOF), f32),
            pltpu.VMEM((rows, DOF), f32),
            pltpu.VMEM((rows, DOF), f32),
            pltpu.VMEM((rows, DOF), bf16),
            pltpu.VMEM((rows, DOF), f32),
        ],
        compiler_params=PARAMS,
        name="cells",
    )((me // 2).astype(jnp.int32).reshape(1), loads[0], pair, above, far, below, held)

    back = lax.all_to_all(solved, "pool", 0, 0, tiled=True)
    fluct, stress, tangent = pl.pallas_call(
        put_kernel,
        out_shape=(
            jax.ShapeDtypeStruct((points, width), bf16),
            jax.ShapeDtypeStruct((RHS, points), f32),
            jax.ShapeDtypeStruct((points, RHS * RHS), f32),
        ),
        in_specs=[VMEM] * 3,
        out_specs=(VMEM,) * 3,
        compiler_params=PARAMS,
        name="put",
    )(place, strain.T, back)
    return fluct, stress.T, tangent


def solution(mesh):
    rows = P(("macro", "pool"), None)
    return jax.shard_map(
        on_device,
        mesh=mesh,
        in_specs=(P("pool", "macro", None), P("pool", None, None), rows, rows, rows, rows),
        out_specs=(rows, rows, rows),
        check_vma=False,
    )
```

```python
import jax
import jax.numpy as jnp
from jax import lax
from jax.experimental import pallas as pl
from jax.experimental.pallas import tpu as pltpu
from jax.sharding import PartitionSpec as P

DOF = 768
RHS = 9
ITERS = 4
CAP = 8
LANES = 128
STRIP = 16
TOGETHER = 3
CHUNKS = 3


VMEM = pl.BlockSpec(memory_space=pltpu.VMEM)
HBM = pl.BlockSpec(memory_space=pltpu.HBM)
SMEM = pl.BlockSpec(memory_space=pltpu.SMEM)
SMALL = pltpu.CompilerParams(vmem_limit_bytes=10 * 2**20)
LARGE = pltpu.CompilerParams(vmem_limit_bytes=28 * 2**20)


def pick_kernel(family_hbm, contact_hbm, previous_hbm, place_ref, sent_hbm,
                contact_ref, previous_ref, sent_ref, family_ref, sems):
    width = RHS * DOF // CHUNKS
    blocks = [slice(k * width, (k + 1) * width) for k in range(CHUNKS)]
    reads = [pltpu.make_async_copy(contact_hbm, contact_ref, sems.at[0])] + [
        pltpu.make_async_copy(previous_hbm.at[:, block], previous_ref.at[:, block], sems.at[1 + k])
        for k, block in enumerate(blocks)
    ]
    named = pltpu.make_async_copy(family_hbm, family_ref, sems.at[2 * (1 + CHUNKS)])
    named.start()
    for copy in reads:
        copy.start()
    named.wait()
    ids = family_ref[...]
    points = ids.shape[1]
    slots = place_ref.shape[0]
    families = slots // CAP
    member = (ids == lax.broadcasted_iota(jnp.int32, (families, points), 0)).astype(jnp.bfloat16)
    earlier = (
        lax.broadcasted_iota(jnp.int32, (points, points), 0)
        < lax.broadcasted_iota(jnp.int32, (points, points), 1)
    ).astype(jnp.bfloat16)
    before = jnp.dot(member, earlier, preferred_element_type=jnp.float32)
    rank = jnp.sum(before * member.astype(jnp.float32), axis=0, keepdims=True)
    slot = ids * CAP + rank.astype(jnp.int32)
    place = (slot == lax.broadcasted_iota(jnp.int32, (slots, points), 0)).astype(jnp.bfloat16)
    place_ref[...] = place

    def take(rows):
        return jnp.dot(place, rows, preferred_element_type=jnp.float32).astype(jnp.bfloat16)

    writes = []
    for k, copy in enumerate(reads):
        copy.wait()
        if k == 0:
            cols = slice(RHS * DOF, (RHS + 1) * DOF)
            sent_ref[:, cols] = take(contact_ref[...].astype(jnp.bfloat16))
        else:
            cols = blocks[k - 1]
            sent_ref[:, cols] = take(previous_ref[:, cols])
        write = pltpu.make_async_copy(sent_ref.at[:, cols], sent_hbm.at[:, cols], sems.at[1 + CHUNKS + k])
        write.start()
        writes.append(write)
    for write in writes:
        write.wait()


def panel_kernel(spot_ref, own_hbm, above_hbm, far_hbm, below_hbm, panel_ref, inverse_ref, sems):
    rows = own_hbm.shape[0]
    count = DOF // rows
    copies = []
    for step, block in enumerate((own_hbm, above_hbm, far_hbm, below_hbm)):
        at = pl.multiple_of(lax.rem(spot_ref[0] + step, count) * rows, rows)
        copies.append(pltpu.make_async_copy(block, panel_ref.at[pl.ds(at, rows), :], sems.at[step]))
    for copy in copies:
        copy.start()
    for copy in copies:
        copy.wait()
    eye = lax.broadcasted_iota(jnp.int32, (LANES, LANES), 0) == lax.broadcasted_iota(
        jnp.int32, (LANES, LANES), 1
    )
    pieces = []
    for k in range(DOF // LANES):
        tile = panel_ref[k * LANES : (k + 1) * LANES, k * LANES : (k + 1) * LANES].astype(jnp.float32)
        pieces.append(jnp.sum(jnp.where(eye, tile, 0.0), axis=0, keepdims=True))
    inverse_ref[...] = 1.0 / jnp.concatenate(pieces, axis=1)


def cells_kernel(load_ref, panel_ref, inverse_ref, points_ref, out_ref,
                 contact_ref, x_ref, r_ref, d_ref, db_ref, p_ref):
    held = points_ref[:, RHS * DOF :].astype(jnp.float32)
    contact_ref[...] = jnp.where(held > 0.0, held, 1.0)
    slots = points_ref.shape[0]
    padded = jnp.concatenate([load_ref[...], jnp.zeros((LANES - RHS, DOF), jnp.float32)], axis=0).astype(
        jnp.bfloat16
    )
    parts = []

    def solve(case):
        base = case * slots
        cols = slice(case * DOF, (case + 1) * DOF)
        whole = slice(base, base + slots)
        p_ref[whole, :] = jnp.dot(points_ref[:, cols], panel_ref[...], preferred_element_type=jnp.float32)
        yield
        currents = []
        for s in range(0, slots, STRIP):
            at = slice(base + s, base + s + STRIP)
            here = slice(s, s + STRIP)
            x = points_ref[here, cols].astype(jnp.float32)
            r = load_ref[case : case + 1, :] - (p_ref[at, :] + contact_ref[here, :] * x)
            d = inverse_ref[...] * r
            currents.append(jnp.sum(r * d, axis=1, keepdims=True))
            r_ref[at, :] = r
            d_ref[at, :] = d
            db_ref[at, :] = d.astype(jnp.bfloat16)
        for sweep in range(ITERS):
            p_ref[whole, :] = jnp.dot(db_ref[whole, :], panel_ref[...], preferred_element_type=jnp.float32)
            yield
            for n, s in enumerate(range(0, slots, STRIP)):
                at = slice(base + s, base + s + STRIP)
                here = slice(s, s + STRIP)
                d = d_ref[at, :]
                image = p_ref[at, :] + contact_ref[here, :] * d
                current = currents[n]
                step = current / (jnp.sum(d * image, axis=1, keepdims=True) + 1e-6)
                x = points_ref[here, cols].astype(jnp.float32) if sweep == 0 else x_ref[at, :]
                x = x + step * d
                if sweep + 1 == ITERS:
                    out_ref[here, cols] = x.astype(jnp.bfloat16)
                    continue
                x_ref[at, :] = x
                r = r_ref[at, :] - step * image
                scaled = inverse_ref[...] * r
                updated = jnp.sum(r * scaled, axis=1, keepdims=True)
                d = scaled + (updated / (current + 1e-6)) * d
                if sweep + 2 < ITERS:
                    r_ref[at, :] = r
                d_ref[at, :] = d
                db_ref[at, :] = d.astype(jnp.bfloat16)
                currents[n] = updated
        part = lax.dot_general(
            out_ref[:, cols], padded, (((1,), (1,)), ((), ())), preferred_element_type=jnp.float32
        )
        parts.append(pltpu.roll(part, case * RHS, 1) if case else part)
        yield

    for first in range(0, RHS, TOGETHER):
        running = [solve(case) for case in range(first, min(first + TOGETHER, RHS))]
        while running:
            running = [one for one in running if next(one, running) is not running]
    out_ref[:, RHS * DOF :] = (sum(parts[1:], parts[0]) * (1.0 / DOF)).astype(jnp.bfloat16)


def put_kernel(place_ref, strain_ref, back_ref, fluct_hbm, stress_ref, tangent_ref, fluct_ref, sems):
    place = place_ref[...]

    def put(rows):
        return lax.dot_general(place, rows, (((0,), (0,)), ((), ())), preferred_element_type=jnp.float32)

    width = RHS * DOF // CHUNKS
    writes = []
    for k in range(CHUNKS):
        cols = slice(k * width, (k + 1) * width)
        fluct_ref[:, cols] = put(back_ref[:, cols]).astype(jnp.bfloat16)
        write = pltpu.make_async_copy(fluct_ref.at[:, cols], fluct_hbm.at[:, cols], sems.at[k])
        write.start()
        writes.append(write)
    tangent = put(back_ref[:, RHS * DOF :])
    entry = lax.broadcasted_iota(jnp.int32, (RHS, LANES), 1)
    index = lax.broadcasted_iota(jnp.int32, (RHS, LANES), 0)
    inside = entry < RHS * RHS
    spread = (inside & (lax.rem(entry, RHS) == index)).astype(jnp.float32)
    gather = (inside & (lax.div(entry, RHS) == index)).astype(jnp.float32)
    strain = lax.dot_general(strain_ref[...], spread, (((0,), (0,)), ((), ())), precision=lax.Precision.HIGHEST)
    stress_ref[...] = lax.dot_general(
        gather, tangent * strain, (((1,), (1,)), ((), ())), precision=lax.Precision.HIGHEST
    )
    tangent_ref[...] = tangent[:, : RHS * RHS]
    for write in writes:
        write.wait()


def far_away(values):
    return pltpu.with_memory_space_constraint(values, pltpu.HBM)


def on_device(panels, loads, family, contact, strain, previous):
    pool = lax.axis_size("pool")
    macro = lax.axis_size("macro")
    points = contact.shape[0]
    slots = pool * CAP
    me = lax.axis_index("macro")
    bf16, f32 = jnp.bfloat16, jnp.float32

    own = panels[0]
    other = lax.ppermute(own, "macro", [(i, i ^ 1) for i in range(macro)])
    pair = jnp.where(
        me % 2 == 0,
        jnp.concatenate([own, other], axis=0),
        jnp.concatenate([other, own], axis=0),
    )
    below, above, far = (
        lax.ppermute(pair, "macro", [(i, (i + shift) % macro) for i in range(macro)]) for shift in (2, -2, 4)
    )

    width = RHS * DOF
    place, sent = pl.pallas_call(
        pick_kernel,
        out_shape=(
            jax.ShapeDtypeStruct((slots, points), bf16),
            pltpu.HBM((slots, width + DOF), bf16),
        ),
        in_specs=[HBM, HBM, HBM],
        out_specs=(VMEM, HBM),
        scratch_shapes=[
            pltpu.VMEM((points, DOF), f32),
            pltpu.VMEM((points, width), bf16),
            pltpu.VMEM((slots, width + DOF), bf16),
            pltpu.VMEM((1, points), jnp.int32),
            pltpu.SemaphoreType.DMA((2 * (1 + CHUNKS) + 1,)),
        ],
        compiler_params=SMALL,
        name="pick",
    )(far_away(family.reshape(1, points)), far_away(contact), far_away(previous))
    held = lax.all_to_all(sent, "pool", 0, 0, tiled=True)

    panel, inverse = pl.pallas_call(
        panel_kernel,
        out_shape=(
            jax.ShapeDtypeStruct((DOF, DOF), bf16),
            jax.ShapeDtypeStruct((1, DOF), f32),
        ),
        in_specs=[SMEM] + [HBM] * 4,
        out_specs=(VMEM,) * 2,
        scratch_shapes=[pltpu.SemaphoreType.DMA((4,))],
        compiler_params=SMALL,
        name="panel",
    )((me // 2).astype(jnp.int32).reshape(1), *map(far_away, (pair, above, far, below)))

    rows = RHS * slots
    solved = pl.pallas_call(
        cells_kernel,
        out_shape=jax.ShapeDtypeStruct((slots, width + LANES), bf16),
        in_specs=[VMEM] * 4,
        out_specs=VMEM,
        scratch_shapes=[
            pltpu.VMEM((slots, DOF), f32),
            pltpu.VMEM((rows, DOF), f32),
            pltpu.VMEM((rows, DOF), f32),
            pltpu.VMEM((rows, DOF), f32),
            pltpu.VMEM((rows, DOF), bf16),
            pltpu.VMEM((rows, DOF), f32),
        ],
        compiler_params=LARGE,
        name="cells",
    )(loads[0], panel, inverse, held)

    back = lax.all_to_all(solved, "pool", 0, 0, tiled=True)
    fluct, stress, tangent = pl.pallas_call(
        put_kernel,
        out_shape=(
            pltpu.HBM((points, width), bf16),
            jax.ShapeDtypeStruct((RHS, points), f32),
            jax.ShapeDtypeStruct((points, RHS * RHS), f32),
        ),
        in_specs=[VMEM] * 3,
        out_specs=(HBM, VMEM, VMEM),
        scratch_shapes=[pltpu.VMEM((points, width), bf16), pltpu.SemaphoreType.DMA((CHUNKS,))],
        compiler_params=SMALL,
        name="put",
    )(place, strain.T, back)
    return fluct, stress.T, tangent


def solution(mesh):
    rows = P(("macro", "pool"), None)
    return jax.shard_map(
        on_device,
        mesh=mesh,
        in_specs=(P("pool", "macro", None), P("pool", None, None), rows, rows, rows, rows),
        out_specs=(rows, rows, rows),
        check_vma=False,
    )
```

```python
import jax
import jax.numpy as jnp
from jax import lax
from jax.experimental import pallas as pl
from jax.experimental.pallas import tpu as pltpu
from jax.sharding import PartitionSpec as P

DOF = 768
RHS = 9
ITERS = 4
CAP = 8
LANES = 128
STRIP = 16
TOGETHER = 3
CHUNKS = 6


VMEM = pl.BlockSpec(memory_space=pltpu.VMEM)
HBM = pl.BlockSpec(memory_space=pltpu.HBM)
SMEM = pl.BlockSpec(memory_space=pltpu.SMEM)
SMALL = pltpu.CompilerParams(vmem_limit_bytes=10 * 2**20)
LARGE = pltpu.CompilerParams(vmem_limit_bytes=28 * 2**20)


def pick_kernel(family_hbm, contact_hbm, previous_hbm, place_ref, sent_hbm,
                contact_ref, previous_ref, sent_ref, family_ref, sems):
    width = RHS * DOF // CHUNKS
    blocks = [slice(k * width, (k + 1) * width) for k in range(CHUNKS)]
    reads = [pltpu.make_async_copy(contact_hbm, contact_ref, sems.at[0])] + [
        pltpu.make_async_copy(previous_hbm.at[:, block], previous_ref.at[:, block], sems.at[1 + k])
        for k, block in enumerate(blocks)
    ]
    named = pltpu.make_async_copy(family_hbm, family_ref, sems.at[2 * (1 + CHUNKS)])
    named.start()
    for copy in reads:
        copy.start()
    named.wait()
    ids = family_ref[...]
    points = ids.shape[1]
    slots = place_ref.shape[0]
    families = slots // CAP
    member = (ids == lax.broadcasted_iota(jnp.int32, (families, points), 0)).astype(jnp.bfloat16)
    earlier = (
        lax.broadcasted_iota(jnp.int32, (points, points), 0)
        < lax.broadcasted_iota(jnp.int32, (points, points), 1)
    ).astype(jnp.bfloat16)
    before = jnp.dot(member, earlier, preferred_element_type=jnp.float32)
    rank = jnp.sum(before * member.astype(jnp.float32), axis=0, keepdims=True)
    slot = ids * CAP + rank.astype(jnp.int32)
    place = (slot == lax.broadcasted_iota(jnp.int32, (slots, points), 0)).astype(jnp.bfloat16)
    place_ref[...] = place

    def take(rows):
        return jnp.dot(place, rows, preferred_element_type=jnp.float32).astype(jnp.bfloat16)

    writes = []
    for k, copy in enumerate(reads):
        copy.wait()
        if k == 0:
            cols = slice(RHS * DOF, (RHS + 1) * DOF)
            sent_ref[:, cols] = take(contact_ref[...].astype(jnp.bfloat16))
        else:
            cols = blocks[k - 1]
            sent_ref[:, cols] = take(previous_ref[:, cols])
        write = pltpu.make_async_copy(sent_ref.at[:, cols], sent_hbm.at[:, cols], sems.at[1 + CHUNKS + k])
        write.start()
        writes.append(write)
    for write in writes:
        write.wait()


def panel_kernel(spot_ref, own_hbm, above_hbm, far_hbm, below_hbm, panel_ref, inverse_ref, sems):
    rows = own_hbm.shape[0]
    count = DOF // rows
    copies = []
    for step, block in enumerate((own_hbm, above_hbm, far_hbm, below_hbm)):
        at = pl.multiple_of(lax.rem(spot_ref[0] + step, count) * rows, rows)
        copies.append(pltpu.make_async_copy(block, panel_ref.at[pl.ds(at, rows), :], sems.at[step]))
    for copy in copies:
        copy.start()
    for copy in copies:
        copy.wait()
    eye = lax.broadcasted_iota(jnp.int32, (LANES, LANES), 0) == lax.broadcasted_iota(
        jnp.int32, (LANES, LANES), 1
    )
    pieces = []
    for k in range(DOF // LANES):
        tile = panel_ref[k * LANES : (k + 1) * LANES, k * LANES : (k + 1) * LANES].astype(jnp.float32)
        pieces.append(jnp.sum(jnp.where(eye, tile, 0.0), axis=0, keepdims=True))
    inverse_ref[...] = 1.0 / jnp.concatenate(pieces, axis=1)


def cells_kernel(load_ref, panel_ref, inverse_ref, points_ref, out_ref,
                 contact_ref, x_ref, r_ref, d_ref, db_ref, p_ref):
    held = points_ref[:, RHS * DOF :].astype(jnp.float32)
    contact_ref[...] = jnp.where(held > 0.0, held, 1.0)
    slots = points_ref.shape[0]
    padded = jnp.concatenate([load_ref[...], jnp.zeros((LANES - RHS, DOF), jnp.float32)], axis=0).astype(
        jnp.bfloat16
    )
    parts = []

    def solve(case):
        base = case * slots
        cols = slice(case * DOF, (case + 1) * DOF)
        whole = slice(base, base + slots)
        p_ref[whole, :] = jnp.dot(points_ref[:, cols], panel_ref[...], preferred_element_type=jnp.float32)
        yield
        currents = []
        for s in range(0, slots, STRIP):
            at = slice(base + s, base + s + STRIP)
            here = slice(s, s + STRIP)
            x = points_ref[here, cols].astype(jnp.float32)
            r = load_ref[case : case + 1, :] - (p_ref[at, :] + contact_ref[here, :] * x)
            d = inverse_ref[...] * r
            currents.append(jnp.sum(r * d, axis=1, keepdims=True))
            r_ref[at, :] = r
            d_ref[at, :] = d
            db_ref[at, :] = d.astype(jnp.bfloat16)
        for sweep in range(ITERS):
            p_ref[whole, :] = jnp.dot(db_ref[whole, :], panel_ref[...], preferred_element_type=jnp.float32)
            yield
            for n, s in enumerate(range(0, slots, STRIP)):
                at = slice(base + s, base + s + STRIP)
                here = slice(s, s + STRIP)
                d = d_ref[at, :]
                image = p_ref[at, :] + contact_ref[here, :] * d
                current = currents[n]
                step = current / (jnp.sum(d * image, axis=1, keepdims=True) + 1e-6)
                x = points_ref[here, cols].astype(jnp.float32) if sweep == 0 else x_ref[at, :]
                x = x + step * d
                if sweep + 1 == ITERS:
                    out_ref[here, cols] = x.astype(jnp.bfloat16)
                    continue
                x_ref[at, :] = x
                r = r_ref[at, :] - step * image
                scaled = inverse_ref[...] * r
                updated = jnp.sum(r * scaled, axis=1, keepdims=True)
                d = scaled + (updated / (current + 1e-6)) * d
                if sweep + 2 < ITERS:
                    r_ref[at, :] = r
                d_ref[at, :] = d
                db_ref[at, :] = d.astype(jnp.bfloat16)
                currents[n] = updated
        part = lax.dot_general(
            out_ref[:, cols], padded, (((1,), (1,)), ((), ())), preferred_element_type=jnp.float32
        )
        parts.append(pltpu.roll(part, case * RHS, 1) if case else part)
        yield

    for first in range(0, RHS, TOGETHER):
        running = [solve(case) for case in range(first, min(first + TOGETHER, RHS))]
        while running:
            running = [one for one in running if next(one, running) is not running]
    out_ref[:, RHS * DOF :] = (sum(parts[1:], parts[0]) * (1.0 / DOF)).astype(jnp.bfloat16)


def put_kernel(place_ref, strain_ref, back_ref, fluct_ref, stress_ref, tangent_ref):
    place = place_ref[...]

    def put(rows):
        return lax.dot_general(place, rows, (((0,), (0,)), ((), ())), preferred_element_type=jnp.float32)

    fluct_ref[...] = put(back_ref[:, : RHS * DOF]).astype(jnp.bfloat16)
    tangent = put(back_ref[:, RHS * DOF :])
    entry = lax.broadcasted_iota(jnp.int32, (RHS, LANES), 1)
    index = lax.broadcasted_iota(jnp.int32, (RHS, LANES), 0)
    inside = entry < RHS * RHS
    spread = (inside & (lax.rem(entry, RHS) == index)).astype(jnp.float32)
    gather = (inside & (lax.div(entry, RHS) == index)).astype(jnp.float32)
    strain = lax.dot_general(strain_ref[...], spread, (((0,), (0,)), ((), ())), precision=lax.Precision.HIGHEST)
    stress_ref[...] = lax.dot_general(
        gather, tangent * strain, (((1,), (1,)), ((), ())), precision=lax.Precision.HIGHEST
    )
    tangent_ref[...] = tangent[:, : RHS * RHS]


def far_away(values):
    return pltpu.with_memory_space_constraint(values, pltpu.HBM)


def on_device(panels, loads, family, contact, strain, previous):
    pool = lax.axis_size("pool")
    macro = lax.axis_size("macro")
    points = contact.shape[0]
    slots = pool * CAP
    me = lax.axis_index("macro")
    bf16, f32 = jnp.bfloat16, jnp.float32

    own = panels[0]
    other = lax.ppermute(own, "macro", [(i, i ^ 1) for i in range(macro)])
    pair = jnp.where(
        me % 2 == 0,
        jnp.concatenate([own, other], axis=0),
        jnp.concatenate([other, own], axis=0),
    )
    below, above, far = (
        lax.ppermute(pair, "macro", [(i, (i + shift) % macro) for i in range(macro)]) for shift in (2, -2, 4)
    )

    width = RHS * DOF
    place, sent = pl.pallas_call(
        pick_kernel,
        out_shape=(
            jax.ShapeDtypeStruct((slots, points), bf16),
            pltpu.HBM((slots, width + DOF), bf16),
        ),
        in_specs=[HBM, HBM, HBM],
        out_specs=(VMEM, HBM),
        scratch_shapes=[
            pltpu.VMEM((points, DOF), f32),
            pltpu.VMEM((points, width), bf16),
            pltpu.VMEM((slots, width + DOF), bf16),
            pltpu.VMEM((1, points), jnp.int32),
            pltpu.SemaphoreType.DMA((2 * (1 + CHUNKS) + 1,)),
        ],
        compiler_params=SMALL,
        name="pick",
    )(far_away(family.reshape(1, points)), far_away(contact), far_away(previous))
    held = lax.all_to_all(sent, "pool", 0, 0, tiled=True)

    panel, inverse = pl.pallas_call(
        panel_kernel,
        out_shape=(
            jax.ShapeDtypeStruct((DOF, DOF), bf16),
            jax.ShapeDtypeStruct((1, DOF), f32),
        ),
        in_specs=[SMEM] + [HBM] * 4,
        out_specs=(VMEM,) * 2,
        scratch_shapes=[pltpu.SemaphoreType.DMA((4,))],
        compiler_params=SMALL,
        name="panel",
    )((me // 2).astype(jnp.int32).reshape(1), *map(far_away, (pair, above, far, below)))

    rows = RHS * slots
    solved = pl.pallas_call(
        cells_kernel,
        out_shape=jax.ShapeDtypeStruct((slots, width + LANES), bf16),
        in_specs=[VMEM] * 4,
        out_specs=VMEM,
        scratch_shapes=[
            pltpu.VMEM((slots, DOF), f32),
            pltpu.VMEM((rows, DOF), f32),
            pltpu.VMEM((rows, DOF), f32),
            pltpu.VMEM((rows, DOF), f32),
            pltpu.VMEM((rows, DOF), bf16),
            pltpu.VMEM((rows, DOF), f32),
        ],
        compiler_params=LARGE,
        name="cells",
    )(loads[0], panel, inverse, held)

    back = lax.all_to_all(solved, "pool", 0, 0, tiled=True)
    fluct, stress, tangent = pl.pallas_call(
        put_kernel,
        out_shape=(
            jax.ShapeDtypeStruct((points, width), bf16),
            jax.ShapeDtypeStruct((RHS, points), f32),
            jax.ShapeDtypeStruct((points, RHS * RHS), f32),
        ),
        in_specs=[VMEM] * 3,
        out_specs=(VMEM,) * 3,
        compiler_params=SMALL,
        name="put",
    )(place, strain.T, back)
    return fluct, stress.T, tangent


def solution(mesh):
    rows = P(("macro", "pool"), None)
    return jax.shard_map(
        on_device,
        mesh=mesh,
        in_specs=(P("pool", "macro", None), P("pool", None, None), rows, rows, rows, rows),
        out_specs=(rows, rows, rows),
        check_vma=False,
    )
```

```python
import jax
import jax.numpy as jnp
from jax import lax
from jax.experimental import pallas as pl
from jax.experimental.pallas import tpu as pltpu
from jax.sharding import PartitionSpec as P

DOF = 768
RHS = 9
ITERS = 4
CAP = 8
LANES = 128
STRIP = 16
TOGETHER = 3
CHUNKS = 3


VMEM = pl.BlockSpec(memory_space=pltpu.VMEM)
HBM = pl.BlockSpec(memory_space=pltpu.HBM)
SMEM = pl.BlockSpec(memory_space=pltpu.SMEM)
SMALL = pltpu.CompilerParams(vmem_limit_bytes=10 * 2**20)
LARGE = pltpu.CompilerParams(
    vmem_limit_bytes=28 * 2**20
)


def pick_kernel(family_hbm, contact_hbm, previous_hbm, place_ref, sent_hbm,
                contact_ref, previous_ref, sent_ref, family_ref, sems):
    width = RHS * DOF // CHUNKS
    blocks = [slice(k * width, (k + 1) * width) for k in range(CHUNKS)]
    reads = [pltpu.make_async_copy(contact_hbm, contact_ref, sems.at[0])] + [
        pltpu.make_async_copy(previous_hbm.at[:, block], previous_ref.at[:, block], sems.at[1 + k])
        for k, block in enumerate(blocks)
    ]
    named = pltpu.make_async_copy(family_hbm, family_ref, sems.at[2 * (1 + CHUNKS)])
    named.start()
    for copy in reads:
        copy.start()
    named.wait()
    ids = family_ref[...]
    points = ids.shape[1]
    slots = place_ref.shape[0]
    families = slots // CAP
    member = (ids == lax.broadcasted_iota(jnp.int32, (families, points), 0)).astype(jnp.bfloat16)
    earlier = (
        lax.broadcasted_iota(jnp.int32, (points, points), 0)
        < lax.broadcasted_iota(jnp.int32, (points, points), 1)
    ).astype(jnp.bfloat16)
    before = jnp.dot(member, earlier, preferred_element_type=jnp.float32)
    rank = jnp.sum(before * member.astype(jnp.float32), axis=0, keepdims=True)
    slot = ids * CAP + rank.astype(jnp.int32)
    place = (slot == lax.broadcasted_iota(jnp.int32, (slots, points), 0)).astype(jnp.bfloat16)
    place_ref[...] = place

    def take(rows):
        return jnp.dot(place, rows, preferred_element_type=jnp.float32).astype(jnp.bfloat16)

    writes = []
    for k, copy in enumerate(reads):
        copy.wait()
        if k == 0:
            cols = slice(RHS * DOF, (RHS + 1) * DOF)
            sent_ref[:, cols] = take(contact_ref[...].astype(jnp.bfloat16))
        else:
            cols = blocks[k - 1]
            sent_ref[:, cols] = take(previous_ref[:, cols])
        write = pltpu.make_async_copy(sent_ref.at[:, cols], sent_hbm.at[:, cols], sems.at[1 + CHUNKS + k])
        write.start()
        writes.append(write)
    for write in writes:
        write.wait()


def panel_kernel(spot_ref, own_hbm, above_hbm, far_hbm, below_hbm, panel_ref, inverse_ref, sems):
    rows = own_hbm.shape[0]
    count = DOF // rows
    copies = []
    for step, block in enumerate((own_hbm, above_hbm, far_hbm, below_hbm)):
        at = pl.multiple_of(lax.rem(spot_ref[0] + step, count) * rows, rows)
        copies.append(pltpu.make_async_copy(block, panel_ref.at[pl.ds(at, rows), :], sems.at[step]))
    for copy in copies:
        copy.start()
    for copy in copies:
        copy.wait()
    eye = lax.broadcasted_iota(jnp.int32, (LANES, LANES), 0) == lax.broadcasted_iota(
        jnp.int32, (LANES, LANES), 1
    )
    pieces = []
    for k in range(DOF // LANES):
        tile = panel_ref[k * LANES : (k + 1) * LANES, k * LANES : (k + 1) * LANES].astype(jnp.float32)
        pieces.append(jnp.sum(jnp.where(eye, tile, 0.0), axis=0, keepdims=True))
    inverse_ref[...] = 1.0 / jnp.concatenate(pieces, axis=1)


def cells_kernel(load_ref, panel_ref, inverse_ref, points_ref, out_ref,
                 contact_ref, x_ref, r_ref, d_ref, db_ref, p_ref):
    held = points_ref[:, RHS * DOF :].astype(jnp.float32)
    contact_ref[...] = jnp.where(held > 0.0, held, 1.0)
    slots = points_ref.shape[0]
    padded = jnp.concatenate([load_ref[...], jnp.zeros((LANES - RHS, DOF), jnp.float32)], axis=0).astype(
        jnp.bfloat16
    )
    parts = []

    def solve(case):
        base = case * slots
        cols = slice(case * DOF, (case + 1) * DOF)
        whole = slice(base, base + slots)
        p_ref[whole, :] = jnp.dot(points_ref[:, cols], panel_ref[...], preferred_element_type=jnp.float32)
        yield
        currents = []
        for s in range(0, slots, STRIP):
            at = slice(base + s, base + s + STRIP)
            here = slice(s, s + STRIP)
            x = points_ref[here, cols].astype(jnp.float32)
            r = load_ref[case : case + 1, :] - (p_ref[at, :] + contact_ref[here, :] * x)
            d = inverse_ref[...] * r
            currents.append(jnp.sum(r * d, axis=1, keepdims=True))
            r_ref[at, :] = r
            d_ref[at, :] = d
            db_ref[at, :] = d.astype(jnp.bfloat16)
        for sweep in range(ITERS):
            p_ref[whole, :] = jnp.dot(db_ref[whole, :], panel_ref[...], preferred_element_type=jnp.float32)
            yield
            for n, s in enumerate(range(0, slots, STRIP)):
                at = slice(base + s, base + s + STRIP)
                here = slice(s, s + STRIP)
                d = d_ref[at, :]
                image = p_ref[at, :] + contact_ref[here, :] * d
                current = currents[n]
                step = current / (jnp.sum(d * image, axis=1, keepdims=True) + 1e-6)
                x = points_ref[here, cols].astype(jnp.float32) if sweep == 0 else x_ref[at, :]
                x = x + step * d
                if sweep + 1 == ITERS:
                    out_ref[here, cols] = x.astype(jnp.bfloat16)
                    continue
                x_ref[at, :] = x
                r = r_ref[at, :] - step * image
                scaled = inverse_ref[...] * r
                updated = jnp.sum(r * scaled, axis=1, keepdims=True)
                d = scaled + (updated / (current + 1e-6)) * d
                if sweep + 2 < ITERS:
                    r_ref[at, :] = r
                d_ref[at, :] = d
                db_ref[at, :] = d.astype(jnp.bfloat16)
                currents[n] = updated
        part = lax.dot_general(
            out_ref[:, cols], padded, (((1,), (1,)), ((), ())), preferred_element_type=jnp.float32
        )
        parts.append(pltpu.roll(part, case * RHS, 1) if case else part)
        yield

    for first in range(0, RHS, TOGETHER):
        running = [solve(case) for case in range(first, min(first + TOGETHER, RHS))]
        while running:
            running = [one for one in running if next(one, running) is not running]
    out_ref[:, RHS * DOF :] = (sum(parts[1:], parts[0]) * (1.0 / DOF)).astype(jnp.bfloat16)


def put_kernel(place_ref, strain_ref, back_ref, fluct_ref, stress_ref, tangent_ref):
    place = place_ref[...]

    def put(rows):
        return lax.dot_general(place, rows, (((0,), (0,)), ((), ())), preferred_element_type=jnp.float32)

    fluct_ref[...] = put(back_ref[:, : RHS * DOF]).astype(jnp.bfloat16)
    tangent = put(back_ref[:, RHS * DOF :])
    entry = lax.broadcasted_iota(jnp.int32, (RHS, LANES), 1)
    index = lax.broadcasted_iota(jnp.int32, (RHS, LANES), 0)
    inside = entry < RHS * RHS
    spread = (inside & (lax.rem(entry, RHS) == index)).astype(jnp.float32)
    gather = (inside & (lax.div(entry, RHS) == index)).astype(jnp.float32)
    strain = lax.dot_general(strain_ref[...], spread, (((0,), (0,)), ((), ())), precision=lax.Precision.HIGHEST)
    stress_ref[...] = lax.dot_general(
        gather, tangent * strain, (((1,), (1,)), ((), ())), precision=lax.Precision.HIGHEST
    )
    tangent_ref[...] = tangent[:, : RHS * RHS]


def far_away(values):
    return pltpu.with_memory_space_constraint(values, pltpu.HBM)


def on_device(panels, loads, family, contact, strain, previous):
    pool = lax.axis_size("pool")
    macro = lax.axis_size("macro")
    points = contact.shape[0]
    slots = pool * CAP
    me = lax.axis_index("macro")
    bf16, f32 = jnp.bfloat16, jnp.float32

    own = panels[0]
    other = lax.ppermute(own, "macro", [(i, i ^ 1) for i in range(macro)])
    pair = jnp.where(
        me % 2 == 0,
        jnp.concatenate([own, other], axis=0),
        jnp.concatenate([other, own], axis=0),
    )
    below, above, far = (
        lax.ppermute(pair, "macro", [(i, (i + shift) % macro) for i in range(macro)]) for shift in (2, -2, 4)
    )

    width = RHS * DOF
    place, sent = pl.pallas_call(
        pick_kernel,
        out_shape=(
            jax.ShapeDtypeStruct((slots, points), bf16),
            pltpu.HBM((slots, width + DOF), bf16),
        ),
        in_specs=[HBM, HBM, HBM],
        out_specs=(VMEM, HBM),
        scratch_shapes=[
            pltpu.VMEM((points, DOF), f32),
            pltpu.VMEM((points, width), bf16),
            pltpu.VMEM((slots, width + DOF), bf16),
            pltpu.VMEM((1, points), jnp.int32),
            pltpu.SemaphoreType.DMA((2 * (1 + CHUNKS) + 1,)),
        ],
        compiler_params=SMALL,
        name="pick",
    )(far_away(family.reshape(1, points)), far_away(contact), far_away(previous))
    held = lax.all_to_all(sent, "pool", 0, 0, tiled=True)

    panel, inverse = pl.pallas_call(
        panel_kernel,
        out_shape=(
            jax.ShapeDtypeStruct((DOF, DOF), bf16),
            jax.ShapeDtypeStruct((1, DOF), f32),
        ),
        in_specs=[SMEM] + [HBM] * 4,
        out_specs=(VMEM,) * 2,
        scratch_shapes=[pltpu.SemaphoreType.DMA((4,))],
        compiler_params=SMALL,
        name="panel",
    )((me // 2).astype(jnp.int32).reshape(1), *map(far_away, (pair, above, far, below)))

    rows = RHS * slots
    solved = pl.pallas_call(
        cells_kernel,
        out_shape=jax.ShapeDtypeStruct((slots, width + LANES), bf16),
        in_specs=[VMEM] * 4,
        out_specs=VMEM,
        scratch_shapes=[
            pltpu.VMEM((slots, DOF), f32),
            pltpu.VMEM((rows, DOF), f32),
            pltpu.VMEM((rows, DOF), f32),
            pltpu.VMEM((rows, DOF), f32),
            pltpu.VMEM((rows, DOF), bf16),
            pltpu.VMEM((rows, DOF), f32),
        ],
        compiler_params=LARGE,
        name="cells",
    )(loads[0], panel, inverse, held)

    back = lax.all_to_all(solved, "pool", 0, 0, tiled=True)
    fluct, stress, tangent = pl.pallas_call(
        put_kernel,
        out_shape=(
            jax.ShapeDtypeStruct((points, width), bf16),
            jax.ShapeDtypeStruct((RHS, points), f32),
            jax.ShapeDtypeStruct((points, RHS * RHS), f32),
        ),
        in_specs=[VMEM] * 3,
        out_specs=(VMEM,) * 3,
        compiler_params=SMALL,
        name="put",
    )(place, strain.T, back)
    return fluct, stress.T, tangent


def solution(mesh):
    rows = P(("macro", "pool"), None)
    return jax.shard_map(
        on_device,
        mesh=mesh,
        in_specs=(P("pool", "macro", None), P("pool", None, None), rows, rows, rows, rows),
        out_specs=(rows, rows, rows),
        check_vma=False,
    )
```
